256 devices in a mesh: ctx: 32 (over z_lo, x, core), tsp: 4 (over y), dp: 2 (over z_hi).
Axes of the slice: x: 4, y: 4, z: 8 (z_hi: 2, z_lo: 4; z = z_hi * 4 + z_lo), core: 2. Of those that a mesh axis runs over, the one named last changes fastest.
Arguments:
- queries: bfloat16 [2, 16384, 2048], P('dp', 'ctx', 'tsp'), may hold values from -6 to 6
- keys: bfloat16 [2, 16384, 2048], P('dp', 'ctx', 'tsp'), may hold values from -6 to 6
- values: bfloat16 [2, 16384, 2048], P('dp', 'ctx', 'tsp'), may hold values from -6 to 6
- attn_out: bfloat16 [2, 16384, 2048], P('dp', 'ctx', 'tsp'), may hold values from -6 to 6
- out_grad: bfloat16 [2, 16384, 4096], P('dp', ('ctx', 'tsp')), may hold values from -12 to 12
- out_weight: bfloat16 [4096, 2048], P('ctx', 'tsp'), may hold values from -0.09375 to 0.09375
- block_mask: int32 [2, 32, 8, 8], P('dp', 'ctx'), may hold values 0 or 1
Outputs:
- query_grads: bfloat16 [2, 16384, 2048], P('dp', 'ctx', 'tsp')
- key_grads: bfloat16 [2, 16384, 2048], P('dp', 'ctx', 'tsp')
- value_grads: bfloat16 [2, 16384, 2048], P('dp', 'ctx', 'tsp')
- weight_grad: float32 [4096, 2048], P('ctx', 'tsp')
The draws below stay inside these ranges and needn't reach their ends.
Inputs may be any that keep to these rules, and one draw needn't show every extreme that they name: `block_mask`: 1 lets a key block feed a later query block of the same group.
All inputs are finite; a program needn't handle non-finite values.
Results may differ from the reference program's by a relative error of at most 0.0058.
Values may be sent and summed in bfloat16 or wider, within the bound.
A program may use at most 128 MiB of HBM per device.

```python
import math
import jax
import jax.numpy as jnp
from jax import lax

D = 4096
HEADS = 16
HEAD = 128
BLK = 64
GROUP = 512
NB = 8
GROUPS = 32
SEQ = 16384
BATCH = 2
HD = 2048


def with_ends(values, rng, smallest, high):
    place = [jax.random.randint(jax.random.fold_in(rng, axis), (), 0, length) for axis, length in enumerate(values.shape)]
    longest = values.shape.index(max(values.shape))
    neighbour = place[:longest] + [(place[longest] + 1) % values.shape[longest]] + place[longest + 1:]
    return values.at[tuple(place)].set(smallest).at[tuple(neighbour)].set(high)


def strengthened(values, rng, source, target, parts, factor):
    def block_of(position):
        return (jnp.arange(values.shape[position]) // (values.shape[position] // parts)).reshape((-1,) + (1,) * (values.ndim - 1 - position))

    near = jax.random.permutation(rng, parts)[block_of(target)]
    other_side = (block_of(target) + parts // 2) % parts
    return jnp.where((block_of(source) == near) | (block_of(source) == other_side), factor * values, values)


def level_of(own_key, dims, split, least, largest):
    level = 1.0
    for axis_at, blocks in split:
        steps = jax.random.uniform(jax.random.fold_in(jax.random.fold_in(own_key, 6), axis_at), (blocks,), jnp.float32, least / len(split), largest / len(split))
        level = level * jnp.repeat(jnp.exp(steps), dims[axis_at] // blocks).reshape((-1,) + (1,) * (len(dims) - 1 - axis_at))
    return level


def gaussian(rng, extent, scale, bound, split=(), held_as=jnp.bfloat16):
    result = scale * jax.random.normal(rng, extent, jnp.float32)
    if split:
        result = result * level_of(rng, extent, split, -0.22, 0.18)
    return jnp.clip(result, -bound, bound).astype(held_as)


def noise_with(rng, shape, scale, reach, pieces, heavy, kind=jnp.bfloat16):
    entries = scale * jax.random.normal(rng, shape, jnp.float32)
    if pieces:
        entries = entries * level_of(rng, shape, pieces, -0.22, 0.18)
    return jnp.clip(strengthened(entries, jax.random.fold_in(rng, 3), *heavy), -reach, reach).astype(kind)


def setup_inputs(seed: int = 0) -> dict:
    key_list = jax.random.split(jax.random.key(seed), 8)
    return {
        "queries": gaussian(key_list[0], (BATCH, SEQ, HD), 1.0, 6.0, ((0, 2), (1, 32), (2, 4))),
        "keys": gaussian(key_list[1], (BATCH, SEQ, HD), 1.0, 6.0, ((0, 2), (1, 32), (2, 4))),
        "values": gaussian(key_list[2], (BATCH, SEQ, HD), 1.0, 6.0, ((0, 2), (1, 32), (2, 4))),
        "attn_out": gaussian(key_list[3], (BATCH, SEQ, HD), 1.0, 6.0, ((0, 2), (1, 32), (2, 4))),
        "out_grad": noise_with(key_list[4], (BATCH, SEQ, D), 0.5, 12.0, ((0, 2), (1, 128)), (1, 2, 128, 5.5)),
        "out_weight": gaussian(key_list[5], (D, HD), D ** -0.5, 0.09375, ((0, 32), (1, 4))),
        "block_mask": with_ends((jax.random.randint(key_list[6], (BATCH, GROUPS, NB, NB), 0, 2) < 1).astype(jnp.int32), jax.random.fold_in(key_list[6], 1), 0, 1),
    }


def allowed_pairs(block_table):
    blocks = block_table.shape[0]
    length = blocks * BLK
    wide_table = jnp.broadcast_to(block_table[:, None, :, None], (blocks, BLK, blocks, BLK)).reshape(length, length)
    row_pos = jnp.arange(length)[:, None]
    col_pos = jnp.arange(length)[None, :]
    row_blk = row_pos // BLK
    col_blk = col_pos // BLK
    return (row_blk > col_blk) & (wide_table == 1) | (row_blk == col_blk) & (row_pos >= col_pos)

def reference(queries, keys, values, attn_out, out_grad, out_weight, block_mask):
    f32 = jnp.float32
    score_scale = 1.0 / math.sqrt(HEAD * SEQ)
    flat_grad = out_grad.reshape(BATCH * SEQ, D)
    out_grads = jnp.dot(flat_grad, out_weight, preferred_element_type=f32).astype(jnp.bfloat16)
    weight_grad = jnp.dot(flat_grad.T, attn_out.reshape(BATCH * SEQ, HEADS * HEAD), preferred_element_type=f32) / math.sqrt(BATCH * SEQ)
    shape_five = (BATCH, GROUPS, GROUP, HEADS, HEAD)
    query_five = queries.reshape(shape_five)
    key_five = keys.reshape(shape_five)
    value_five = values.reshape(shape_five)
    grad_five = out_grads.reshape(shape_five)
    key_value = jnp.einsum('bcthd,bcthe->bchde', key_five.astype(f32), value_five.astype(f32))
    query_grad = jnp.einsum('bcthd,bcthe->bchde', query_five.astype(f32), grad_five.astype(f32))
    earlier_sum = jnp.cumsum(key_value, axis=1) - key_value
    later_sum = jnp.flip(jnp.cumsum(jnp.flip(query_grad, 1), axis=1), 1) - query_grad
    prev_state = (earlier_sum * score_scale).astype(jnp.bfloat16)
    later_state = (later_sum * score_scale).astype(jnp.bfloat16)
    items = BATCH * GROUPS
    shape_four = (items, GROUP, HEADS, HEAD)
    state_shape = (items, HEADS, HEAD, HEAD)
    stacked = (query_five.reshape(shape_four), key_five.reshape(shape_four), value_five.reshape(shape_four), grad_five.reshape(shape_four), prev_state.reshape(state_shape), later_state.reshape(state_shape), block_mask.reshape(items, NB, NB))

    def one_group(item):
        query_here, key_here, value_here, grad_here, prev_here, later_here, table_here = item
        allowed = allowed_pairs(table_here)
        query_f = query_here.astype(f32)
        key_f = key_here.astype(f32)
        value_f = value_here.astype(f32)
        grad_f = grad_here.astype(f32)
        scores = jnp.einsum('thd,shd->hts', query_f, key_f) * score_scale
        score_weights = jnp.where(allowed[None], scores, 0.0).astype(jnp.bfloat16).astype(f32)
        mixing = jnp.einsum('the,she->hts', grad_f, value_f) * score_scale
        grad_weights = jnp.where(allowed[None], mixing, 0.0).astype(jnp.bfloat16).astype(f32)
        prev_f = prev_here.astype(f32)
        later_f = later_here.astype(f32)
        query_out = jnp.einsum('hts,shd->thd', grad_weights, key_f) + jnp.einsum('the,hde->thd', grad_f, prev_f)
        key_out = jnp.einsum('hts,thd->shd', grad_weights, query_f) + jnp.einsum('she,hde->shd', value_f, later_f)
        value_out = jnp.einsum('hts,the->she', score_weights, grad_f) + jnp.einsum('shd,hde->she', key_f, later_f)
        return (query_out.astype(jnp.bfloat16), key_out.astype(jnp.bfloat16), value_out.astype(jnp.bfloat16))
    query_grads, key_grads, value_grads = lax.map(one_group, stacked)
    out_shape = (BATCH, SEQ, HEADS * HEAD)
    return (query_grads.reshape(out_shape), key_grads.reshape(out_shape), value_grads.reshape(out_shape), weight_grad)
```

```python
import math

import jax
import jax.numpy as jnp
from jax import lax
from jax.experimental import pallas as pl
from jax.experimental.pallas import tpu as pltpu
from jax.sharding import PartitionSpec as P

HEAD = 128
BLK = 64
MESH = pl.DeviceIdType.MESH
BF = jnp.bfloat16
F32 = jnp.float32
NT = (((1,), (1,)), ((), ()))
OFFSETS = (0, 3, 1, 2)


def mm(a, b):
    return jnp.dot(a, b, preferred_element_type=F32)


def mm_nt(a, b):
    return lax.dot_general(a, b, NT, preferred_element_type=F32)


def kernel(score_scale, norm_factor,
           q_hbm, k_hbm, v_hbm, a_hbm, g_hbm, w_hbm, bm_ref,
           qo_ref, ko_ref, vo_ref, wg_ref,
           q, k, v, qt, kt, og, gp, wh, ab, att, ms, mst, st,
           dacc, drecv, do, wgf, sb, rb, pz, sz, rz,
           s_own, s_sib, s_x, r_x, s_z, r_z, s_out, state, sbase,
           qacc, kacc, vacc, lsem, ssem, rsem):
    i = lax.axis_index("ctx")
    y = lax.axis_index("tsp")
    zh = lax.axis_index("dp")
    c = lax.rem(i, 2)
    x = lax.rem(i // 2, 4)
    zl = i // 8
    oc = 1 - c
    s = 1 - 2 * c

    def dev(zl_=None, x_=None, c_=None, y_=None, zh_=None):
        zl_ = zl if zl_ is None else zl_
        x_ = x if x_ is None else x_
        c_ = c if c_ is None else c_
        y_ = y if y_ is None else y_
        zh_ = zh if zh_ is None else zh_
        return ((zl_ * 4 + x_) * 2 + c_, y_, zh_)

    def m4(e):
        return lax.rem(e + 8, 4)

    def zring(d):
        z = lax.rem(zh * 4 + zl + d + 8, 8)
        return dev(zl_=lax.rem(z, 4), zh_=z // 4)

    sibling = dev(c_=oc)
    count = [0]
    sent = []

    def remote(src, dst, device):
        n = count[0]
        count[0] += 1
        copy = pltpu.make_async_remote_copy(
            src_ref=src, dst_ref=dst, send_sem=ssem.at[n], recv_sem=rsem.at[n],
            device_id=device, device_id_type=MESH)
        copy.start()
        sent.append(copy)
        return copy

    lcount = [0]

    def local(src, dst):
        n = lcount[0]
        lcount[0] += 1
        copy = pltpu.make_async_copy(src, dst, lsem.at[n])
        copy.start()
        return copy

    def chunk_of(j, core):
        return m4(zl - (1 - 2 * core) * OFFSETS[j])

    def load_g(j):
        out = []
        for core, dst in ((c, og.at[j, c, y]), (oc, gp.at[j])):
            kk = chunk_of(j, core)
            for m in range(4):
                col = pl.multiple_of(((kk * 4 + m) * 2 + core) * 128, 128)
                out.append(local(g_hbm.at[:, pl.ds(col, 128)], dst.at[:, pl.ds(m * 128, 128)]))
        return out

    lw = local(w_hbm, wh.at[zl, x])
    lg = [load_g(j) for j in range(4)]
    lk = local(k_hbm, k)
    lv = local(v_hbm, v)
    lq = local(q_hbm, q)
    la = local(a_hbm, ab.at[c])

    up, down = m4(y + 1), m4(y - 1)
    peers = [sibling]
    for yy in (up, down):
        peers += [dev(y_=yy), dev(y_=yy, c_=oc)]
    peers += [dev(x_=m4(x + d)) for d in (1, 2, 3)]
    peers += [zring(1), zring(-1)]
    peers += [dev(zl_=m4(zl + d)) for d in (1, 2, 3)]
    barrier = pltpu.get_barrier_semaphore()
    for peer in peers:
        pl.semaphore_signal(barrier, inc=1, device_id=peer, device_id_type=MESH)
    pl.semaphore_wait(barrier, len(peers))

    lo, hi = pl.ds(0, 64), pl.ds(64, 64)
    lw.wait()
    wx = [remote(wh.at[zl, x, lo], wh.at[zl, x, lo], dev(x_=m4(x + d * s))) for d in (1, -1)]
    wz = [remote(wh.at[zl, x, hi], wh.at[zl, x, hi], zring(d * s)) for d in (1, -1)]

    def send_g(j):
        for cp in lg[j]:
            cp.wait()
        own, other = og.at[j, c, y], gp.at[j]
        return {
            "same+": remote(own, own, dev(y_=up)),
            "same-": remote(own, own, dev(y_=down)),
            "cross+": remote(other, own, dev(y_=up, c_=oc)),
            "cross-": remote(other, own, dev(y_=down, c_=oc)),
            "sib": remote(other, own, sibling),
        }

    def forward_g(j):
        yc = yg[j]
        yc["same+"].wait_recv()
        a = og.at[j, c, down]
        fa = remote(a, a, dev(y_=up))
        yc["cross-"].wait_recv()
        b = og.at[j, oc, up]
        fb = remote(b, b, dev(y_=down))
        yc["fa"], yc["fb"] = fa, fb

    def finish_g(j):
        yc = yg[j]
        for name in ("same-", "cross+", "sib", "fa", "fb"):
            yc[name].wait_recv()

    yg = [send_g(0)]
    lv.wait()
    la.wait()
    ra = remote(ab.at[c], ab.at[c], sibling)
    yg.append(send_g(1))

    sub = lax.broadcasted_iota(jnp.int32, (BLK, 128), 0)
    lane = lax.broadcasted_iota(jnp.int32, (BLK, 128), 1)
    left = lane < BLK
    within = jnp.where(left, lane, lane - BLK)

    def gate(a, b):
        return jnp.where(bm_ref[a, b] == 1, score_scale, 0.0).astype(F32)

    def piece(entry_a, entry_b):
        return jnp.where(left, entry_a, entry_b)

    zero = jnp.zeros((BLK, 128), F32)
    causal = jnp.where(sub >= within, score_scale, 0.0).astype(F32)
    anti = jnp.where(sub <= within, score_scale, 0.0).astype(F32)

    def entry(i_, j_, diagonal):
        if j_ > i_:
            return zero
        if j_ == i_:
            return diagonal
        return jnp.full((BLK, 128), gate(i_, j_))

    for r in range(8):
        for t in range(4):
            ms[pl.ds(r * BLK, BLK), pl.ds(t * 128, 128)] = piece(
                entry(r, 2 * t, causal), entry(r, 2 * t + 1, causal))
            mst[pl.ds(r * BLK, BLK), pl.ds(t * 128, 128)] = piece(
                entry(2 * t, r, anti), entry(2 * t + 1, r, anti))

    wx[0].wait_recv()
    xb = m4(x - s)
    wx.append(remote(wh.at[zl, xb, lo], wh.at[zl, xb, lo], dev(x_=m4(x + s))))
    wz[0].wait_recv()
    zb = m4(zl - s)
    wz.append(remote(wh.at[zb, x, hi], wh.at[zb, x, hi], zring(s)))

    def head(h):
        return pl.ds(h * HEAD, HEAD)

    def scan_start(n):
        there = pl.multiple_of(oc * 256, 256)
        return remote(s_own.at[n, pl.ds(there, 256)], s_sib.at[n], sibling)

    def scan_x(n, first):
        first.wait_recv()
        here = pl.multiple_of(c * 256, 256)
        total = s_own[n, pl.ds(here, 256)] + s_sib[n]
        s_x[n] = total.astype(BF)
        return [remote(s_x.at[n], r_x.at[n, x], dev(x_=m4(x + d))) for d in (1, 2, 3)]

    def scan_z(n, copies, after):
        for cp in copies:
            cp.wait_recv()
        here = pl.multiple_of(c * 256, 256)
        total = s_own[n, pl.ds(here, 256)] + s_sib[n]
        part = jnp.zeros((256, 128), F32)
        for d in (1, 2, 3):
            xo = m4(x + d)
            value = r_x[n, xo].astype(F32)
            total = total + value
            use = xo > x if after else xo < x
            part = part + jnp.where(use, value, 0.0)
        sbase[n] = part
        s_z[n] = total.astype(BF)
        return [remote(s_z.at[n], r_z.at[n, zl], dev(zl_=m4(zl + d))) for d in (1, 2, 3)]

    def scan_end(n, copies, after):
        for cp in copies:
            cp.wait_recv()
        here = pl.ds(pl.multiple_of(c * 256, 256), 256)
        part = sbase[n]
        for d in (1, 2, 3):
            zo = m4(zl + d)
            use = zo > zl if after else zo < zl
            part = part + jnp.where(use, r_z[n, zo].astype(F32), 0.0)
        edge = 0 if after else 1
        mine = part + jnp.where(c == edge, s_sib[n], 0.0)
        theirs = part + jnp.where(oc == edge, s_own[n, here], 0.0)
        s_out[n] = (theirs * score_scale).astype(BF)
        state[n, here] = (mine * score_scale).astype(BF)
        return remote(s_out.at[n], state.at[n, here], sibling)

    lk.wait()
    for h in range(4):
        kt[h] = k[:, head(h)].T
        s_own[0, head(h)] = mm(kt[h], v[:, head(h)])
    kv = scan_start(0)

    wx[1].wait_recv()
    wx[2].wait_recv()
    wzz = [remote(wh.at[zl, :, lo], wh.at[zl, :, lo], zring(d * s)) for d in (1, -1)]
    wz[1].wait_recv()
    wz[2].wait_recv()
    wxx = [remote(wh.at[:, x, hi], wh.at[:, x, hi], dev(x_=m4(x + d * s))) for d in (1, -1)]

    forward_g(0)
    yg.append(send_g(2))
    kv = scan_x(0, kv)
    lq.wait()
    for h in range(4):
        qt[h] = q[:, head(h)].T
    ra.wait_recv()
    for g in range(2):
        for t in range(4):
            att[pl.ds(t * 128, 128), pl.ds(g * 512, 512)] = ab[g, :, pl.ds(t * 128, 128)].T

    wzz[0].wait_recv()
    wzz.append(remote(wh.at[zb, :, lo], wh.at[zb, :, lo], zring(s)))
    wxx[0].wait_recv()
    wxx.append(remote(wh.at[:, xb, hi], wh.at[:, xb, hi], dev(x_=m4(x + s))))

    def weight_chunk(j):
        rhs = og[j].reshape(1024, 512)
        for m in range(4):
            full = mm(att[...], rhs[:, m * 128:(m + 1) * 128]) * norm_factor
            wgf[j, m] = full

    def grads_chunk(j):
        kk = chunk_of(j, c)
        rhs = wh[kk].reshape(512, 512)
        for g in range(2):
            part = mm(og[j, g].reshape(512, 512), rhs)
            if j == 0:
                dacc[g] = part
            else:
                dacc[g] = dacc[g] + part

    xs = {}

    def xs_first(j):
        sb[j, 0] = wgf[j, m4(x + 2)].astype(BF)
        first = remote(sb.at[j, 0], rb.at[j, 0], dev(x_=m4(x + s)))
        sb[j, 1] = wgf[j, m4(x - s)].astype(BF)
        second = remote(sb.at[j, 1], rb.at[j, 1], dev(x_=m4(x - s)))
        xs[j] = [first, second]

    def xs_second(j):
        xs[j][0].wait_recv()
        sb[j, 2] = (rb[j, 0].astype(F32) + wgf[j, m4(x + s)]).astype(BF)
        xs[j].append(remote(sb.at[j, 2], rb.at[j, 2], dev(x_=m4(x + s))))

    def xs_end(j):
        xs[j][1].wait_recv()
        xs[j][2].wait_recv()
        pz[j] = wgf[j, x] + rb[j, 1].astype(F32) + rb[j, 2].astype(F32)

    zs = {}

    def z_send(n, j, before, direction):
        value = pz[j]
        if before is not None:
            zs[before].wait_recv()
            value = value + rz[before].astype(F32)
        sz[n] = value.astype(BF)
        zs[n] = remote(sz.at[n], rz.at[n], zring(direction * s))

    def scores(h):
        st[h] = (mm_nt(k[:, head(h)], q[:, head(h)]) * mst[...]).astype(BF)

    finish_g(0)
    weight_chunk(0)
    xs_first(0)
    for cp in wzz[1:] + wxx[1:]:
        cp.wait_recv()
    grads_chunk(0)
    kv = scan_z(0, kv, False)
    forward_g(1)
    yg.append(send_g(3))
    scores(0)
    scores(1)
    finish_g(1)
    weight_chunk(1)
    xs_first(1)
    xs_second(0)
    grads_chunk(1)
    kv = scan_end(0, kv, False)
    forward_g(2)
    scores(2)
    scores(3)
    xs_end(0)
    z_send(0, 0, None, -1)
    finish_g(2)
    weight_chunk(2)
    xs_first(2)
    xs_second(1)
    grads_chunk(2)
    forward_g(3)
    xs_end(1)
    z_send(1, 1, 0, -1)
    xs_second(2)
    finish_g(3)
    grads_chunk(3)
    exchange = remote(dacc.at[oc], drecv, sibling)
    weight_chunk(3)
    xs_first(3)
    exchange.wait_recv()
    do[...] = (dacc[c] + drecv[...]).astype(BF)
    for h in range(4):
        s_own[1, head(h)] = mm(qt[h], do[:, head(h)])
    qg = scan_start(1)
    xs_end(2)
    z_send(4, 2, None, 1)

    def local_part(h):
        cols = head(h)
        dh = do[:, cols]
        gw = (mm_nt(dh, v[:, cols]) * ms[...]).astype(BF)
        qacc[:, cols] = mm(gw, k[:, cols])
        gt = (mm_nt(v[:, cols], dh) * mst[...]).astype(BF)
        kacc[:, cols] = mm(gt, q[:, cols])
        vacc[:, cols] = mm(st[h], dh)

    local_part(0)
    qg = scan_x(1, qg)
    local_part(1)
    xs_second(3)
    local_part(2)
    qg = scan_z(1, qg, True)
    local_part(3)
    xs_end(3)
    z_send(2, 3, 1, -1)
    z_send(5, 3, 4, 1)
    kv.wait_recv()
    for h in range(4):
        cols = head(h)
        qo_ref[:, cols] = (qacc[:, cols] + mm_nt(do[:, cols], state[0, cols])).astype(BF)
    qg = scan_end(1, qg, True)
    z_send(3, 2, 2, -1)
    z_send(6, 1, 5, 1)
    qg.wait_recv()
    for h in range(4):
        cols = head(h)
        ko_ref[:, cols] = (kacc[:, cols] + mm_nt(v[:, cols], state[1, cols])).astype(BF)
        vo_ref[:, cols] = (vacc[:, cols] + mm(k[:, cols], state[1, cols])).astype(BF)
    zs[3].wait_recv()
    zs[6].wait_recv()
    wg_ref[...] = (pz[0] + rz[3].astype(F32) + rz[6].astype(F32)).T
    for cp in sent:
        cp.wait_send()


def shards(queries, keys, values, attn_out, out_grad, out_weight, block_mask):
    group_len, width = queries.shape[1:]
    seq_len = group_len * lax.axis_size("ctx")
    score_scale = 1.0 / math.sqrt(HEAD * seq_len)
    norm_factor = 1.0 / math.sqrt(seq_len * lax.axis_size("dp"))
    tokens, model = out_grad.shape[1:]
    V = pltpu.VMEM
    square = (group_len, width)
    any_spec = pl.BlockSpec(memory_space=pl.ANY)
    vmem_spec = pl.BlockSpec(memory_space=pltpu.VMEM)
    body = lambda *refs: kernel(score_scale, norm_factor, *refs)
    out = pl.pallas_call(
        body,
        out_shape=(
            jax.ShapeDtypeStruct(square, BF),
            jax.ShapeDtypeStruct(square, BF),
            jax.ShapeDtypeStruct(square, BF),
            jax.ShapeDtypeStruct(out_weight.shape, F32),
        ),
        in_specs=[any_spec] * 6 + [pl.BlockSpec(memory_space=pltpu.SMEM)],
        out_specs=(vmem_spec,) * 4,
        scratch_shapes=[
            V(square, BF), V(square, BF), V(square, BF),
            V((4, 128, 512), BF), V((4, 128, 512), BF),
            V((4, 2, 4, 128, 512), BF), V((4, 128, 512), BF),
            V((4, 4, 128, 512), BF),
            V((2, 512, 512), BF), V((512, 1024), BF),
            V(square, F32), V(square, F32), V((4, 512, 512), BF),
            V((2, 512, 512), F32), V(square, F32), V(square, BF),
            V((4, 4, 512, 128), F32), V((4, 3, 512, 128), BF), V((4, 3, 512, 128), BF),
            V((4, 512, 128), F32), V((7, 512, 128), BF), V((7, 512, 128), BF),
            V((2, 512, 128), F32), V((2, 256, 128), F32),
            V((2, 256, 128), BF), V((2, 4, 256, 128), BF),
            V((2, 256, 128), BF), V((2, 4, 256, 128), BF),
            V((2, 256, 128), BF), V((2, 512, 128), BF), V((2, 256, 128), F32),
            V(square, F32), V(square, F32), V(square, F32),
            pltpu.SemaphoreType.DMA((40,)),
            pltpu.SemaphoreType.DMA((96,)),
            pltpu.SemaphoreType.DMA((96,)),
        ],
        compiler_params=pltpu.CompilerParams(
            collective_id=0, has_side_effects=True, vmem_limit_bytes=58 << 20),
        name="layer_backward",
    )(queries[0], keys[0], values[0], attn_out[0], out_grad[0], out_weight, block_mask[0, 0])
    return out[0][None], out[1][None], out[2][None], out[3]


def solution(mesh):
    placed = (
        P("dp", "ctx", "tsp"),
        P("dp", "ctx", "tsp"),
        P("dp", "ctx", "tsp"),
        P("dp", "ctx", "tsp"),
        P("dp", ("ctx", "tsp"), None),
        P("ctx", "tsp"),
        P("dp", "ctx", None, None),
    )
    return jax.shard_map(
        shards,
        mesh=mesh,
        in_specs=placed,
        out_specs=(
            P("dp", "ctx", "tsp"),
            P("dp", "ctx", "tsp"),
            P("dp", "ctx", "tsp"),
            P("ctx", "tsp"),
        ),
        check_vma=False,
    )
```

```python
import math

import jax
import jax.numpy as jnp
from jax import lax
from jax.experimental import pallas as pl
from jax.experimental.pallas import tpu as pltpu
from jax.sharding import PartitionSpec as P

HEAD = 128
BLK = 64
MESH = pl.DeviceIdType.MESH
BF = jnp.bfloat16
F32 = jnp.float32
NT = (((1,), (1,)), ((), ()))
OFFSETS = (0, 3, 1, 2)
SENDS = ((1,), (2,), (3, 4, 5), (), (), ())
PARTS = ((0, 0, 4), (1, 0, 4), (2, 0, 4), (3, 0, 2), (3, 2, 3), (3, 3, 4))


def mm(a, b):
    return jnp.dot(a, b, preferred_element_type=F32)


def mm_nt(a, b):
    return lax.dot_general(a, b, NT, preferred_element_type=F32)


def kernel(score_scale, norm_factor,
           q_hbm, k_hbm, v_hbm, a_hbm, g_hbm, w_hbm, bm_ref,
           qo_hbm, ko_hbm, vo_hbm, wg_hbm,
           q, k, v, qt, kt, og, gp, wh, ab, att, ms, mst, st,
           dacc, drecv, do, wgf, sb, rb, pz, sz, rz,
           s_own, s_sib, s_x, r_x, r_q, s_z, r_z, s_u, r_u, s_out, near, state,
           qacc, kacc, vacc, qo, ko, vo, wg, lsem, ssem, rsem):
    i = lax.axis_index("ctx")
    y = lax.axis_index("tsp")
    zh = lax.axis_index("dp")
    c = lax.rem(i, 2)
    x = lax.rem(i // 2, 4)
    zl = i // 8
    oc = 1 - c
    s = 1 - 2 * c

    def dev(zl_=None, x_=None, c_=None, y_=None, zh_=None):
        zl_ = zl if zl_ is None else zl_
        x_ = x if x_ is None else x_
        c_ = c if c_ is None else c_
        y_ = y if y_ is None else y_
        zh_ = zh if zh_ is None else zh_
        return ((zl_ * 4 + x_) * 2 + c_, y_, zh_)

    def m4(e):
        return lax.rem(e + 8, 4)

    def zring(d):
        z = lax.rem(zh * 4 + zl + d + 8, 8)
        return dev(zl_=lax.rem(z, 4), zh_=z // 4)

    sibling = dev(c_=oc)
    count = [0]
    sent = []

    def remote(src, dst, device):
        n = count[0]
        count[0] += 1
        copy = pltpu.make_async_remote_copy(
            src_ref=src, dst_ref=dst, send_sem=ssem.at[n], recv_sem=rsem.at[n],
            device_id=device, device_id_type=MESH)
        copy.start()
        sent.append(copy)
        return copy

    lcount = [0]

    def local(src, dst):
        n = lcount[0]
        lcount[0] += 1
        copy = pltpu.make_async_copy(src, dst, lsem.at[n])
        copy.start()
        return copy

    def chunk_of(j, core):
        return m4(zl - (1 - 2 * core) * OFFSETS[j])

    def x_of(p, core):
        side = 1 - 2 * core
        return m4(x + (2, -side, side, 0)[p])

    def load_g(n):
        j, p0, p1 = PARTS[n]
        out = []
        for core, dst in ((c, og.at[j, c, y]), (oc, gp.at[j])):
            kk = chunk_of(j, core)
            for p in range(p0, p1):
                col = pl.multiple_of(((kk * 4 + x_of(p, core)) * 2 + core) * 128, 128)
                out.append(local(g_hbm.at[:, pl.ds(col, 128)], dst.at[:, pl.ds(p * 128, 128)]))
        return out

    lw = local(w_hbm, wh.at[zl, x])
    lg = [load_g(n) for n in range(len(PARTS))]
    lk = local(k_hbm, k)
    lv = local(v_hbm, v)
    lq = local(q_hbm, q)
    la = local(a_hbm, ab.at[c])

    up, down = m4(y + 1), m4(y - 1)
    peers = [sibling]
    for yy in (up, down):
        peers += [dev(y_=yy), dev(y_=yy, c_=oc)]
    peers += [dev(x_=m4(x + d), c_=cc) for d in (1, 2, 3) for cc in (c, oc)]
    peers += [zring(d) for d in (1, -1, 2, -2, 3, -3)]
    barrier = pltpu.get_barrier_semaphore()
    for peer in peers:
        pl.semaphore_signal(barrier, inc=1, device_id=peer, device_id_type=MESH)
    pl.semaphore_wait(barrier, len(peers))

    def send_g(n):
        for cp in lg[n]:
            cp.wait()
        j, p0, p1 = PARTS[n]
        cols = pl.ds(p0 * 128, (p1 - p0) * 128)
        own, other = og.at[j, c, y, :, cols], gp.at[j, :, cols]
        return {
            "same+": remote(own, own, dev(y_=up)),
            "cross-": remote(other, own, dev(y_=down, c_=oc)),
            "cross+": remote(other, own, dev(y_=up, c_=oc)),
            "same-": remote(own, own, dev(y_=down)),
            "sib": remote(other, own, sibling),
        }

    yg = []

    def forward_g(n):
        j, p0, p1 = PARTS[n]
        cols = pl.ds(p0 * 128, (p1 - p0) * 128)
        yc = yg[n]
        yc["same+"].wait_recv()
        a = og.at[j, c, down, :, cols]
        yc["fa"] = remote(a, a, dev(y_=up))
        yc["cross-"].wait_recv()
        b = og.at[j, oc, up, :, cols]
        yc["fb"] = remote(b, b, dev(y_=down))
        for later in SENDS[n]:
            yg.append(send_g(later))

    def finish_g(n):
        for name in ("same-", "cross+", "sib", "fa", "fb"):
            yg[n][name].wait_recv()

    yg.append(send_g(0))

    lo, hi = pl.ds(0, 64), pl.ds(64, 64)
    lw.wait()
    wx = [remote(wh.at[zl, x, lo], wh.at[zl, x, lo], dev(x_=m4(x + d * s))) for d in (1, -1)]
    wz = [remote(wh.at[zl, x, hi], wh.at[zl, x, hi], zring(d * s)) for d in (1, -1)]

    la.wait()
    ra = remote(ab.at[c], ab.at[c], sibling)

    sub = lax.broadcasted_iota(jnp.int32, (BLK, 128), 0)
    lane = lax.broadcasted_iota(jnp.int32, (BLK, 128), 1)
    left = lane < BLK
    within = jnp.where(left, lane, lane - BLK)

    def gate(a, b):
        return jnp.where(bm_ref[a, b] == 1, score_scale, 0.0).astype(F32)

    def piece(entry_a, entry_b):
        return jnp.where(left, entry_a, entry_b)

    zero = jnp.zeros((BLK, 128), F32)
    causal = jnp.where(sub >= within, score_scale, 0.0).astype(F32)
    anti = jnp.where(sub <= within, score_scale, 0.0).astype(F32)

    def entry(i_, j_, diagonal):
        if j_ > i_:
            return zero
        if j_ == i_:
            return diagonal
        return jnp.full((BLK, 128), gate(i_, j_))

    for r in range(8):
        for t in range(4):
            ms[pl.ds(r * BLK, BLK), pl.ds(t * 128, 128)] = piece(
                entry(r, 2 * t, causal), entry(r, 2 * t + 1, causal))
            mst[pl.ds(r * BLK, BLK), pl.ds(t * 128, 128)] = piece(
                entry(2 * t, r, anti), entry(2 * t + 1, r, anti))

    def head(h):
        return pl.ds(h * HEAD, HEAD)

    here = pl.ds(pl.multiple_of(c * 256, 256), 256)
    there = pl.ds(pl.multiple_of(oc * 256, 256), 256)
    me = 2 * x + c
    row = [(x, oc)] + [(m4(x + d), cc) for d in (1, 2, 3) for cc in (c, oc)]

    def eighth(at):
        return pl.ds(pl.multiple_of(at * 64, 64), 64)

    def scan_start(n):
        out = {"sib": remote(s_own.at[n, there], s_sib.at[n], sibling)}
        out["row"] = [
            remote(s_own.at[n, eighth(2 * xo + co)], r_q.at[n, me], dev(x_=xo, c_=co))
            for xo, co in row]
        return out

    def scan_x(n, cps):
        cps["sib"].wait_recv()
        s_x[n] = (s_own[n, here] + s_sib[n]).astype(BF)
        cps["x"] = [remote(s_x.at[n], r_x.at[n, x], dev(x_=m4(x + d))) for d in (1, 2, 3)]

    def scan_z(n, cps):
        for cp in cps["row"]:
            cp.wait_recv()
        total = s_own[n, eighth(me)]
        for xo, co in row:
            total = total + r_q[n, 2 * xo + co]
        s_z[n] = total.astype(BF)
        cps["z"] = [remote(s_z.at[n], r_z.at[n, zl], dev(zl_=m4(zl + d))) for d in (1, 2, 3)]

    def scan_h(n, cps, after):
        for cp in cps["x"]:
            cp.wait_recv()
        part = jnp.zeros((256, 128), F32)
        for d in (1, 2, 3):
            xo = m4(x + d)
            use = xo > x if after else xo < x
            part = part + jnp.where(use, r_x[n, xo].astype(F32), 0.0)
        edge = 0 if after else 1
        s_out[n] = part + jnp.where(oc == edge, s_own[n, here], 0.0)
        cps["half"] = remote(s_out.at[n], near.at[n, here], sibling)
        near[n, here] = part + jnp.where(c == edge, s_sib[n], 0.0)

    def scan_u(n, cps, after):
        for cp in cps["z"]:
            cp.wait_recv()
        part = jnp.zeros((64, 128), F32)
        for d in (1, 2, 3):
            zo = m4(zl + d)
            use = zo > zl if after else zo < zl
            part = part + jnp.where(use, r_z[n, zo].astype(F32), 0.0)
        s_u[n] = part
        cps["u"] = [remote(s_u.at[n], r_u.at[n, me], dev(x_=xo, c_=co)) for xo, co in row]
        r_u[n, me] = part

    def scan_end(n, cps):
        cps["half"].wait_recv()
        for cp in cps["u"]:
            cp.wait_recv()
        state[n] = ((near[n] + r_u[n].reshape(512, 128)) * score_scale).astype(BF)

    def weight_part(n):
        j, p0, p1 = PARTS[n]
        rhs = og[j, :, :, :, p0 * 128:p1 * 128].reshape(1024, (p1 - p0) * 128)
        full = mm(att[...], rhs) * norm_factor
        for p in range(p0, p1):
            wgf[j, p] = full[:, (p - p0) * 128:(p - p0 + 1) * 128]

    def grads_part(n):
        j, p0, p1 = PARTS[n]
        kk = chunk_of(j, c)
        rhs = jnp.concatenate([wh[kk, x_of(p, c)] for p in range(p0, p1)], axis=0)
        for g in range(2):
            part = mm(og[j, g, :, :, p0 * 128:p1 * 128].reshape(512, (p1 - p0) * 128), rhs)
            if n == 0:
                dacc[g] = part
            else:
                dacc[g] = dacc[g] + part

    xs = {}

    def xs_first(j):
        sb[j, 0] = wgf[j, 0].astype(BF)
        first = remote(sb.at[j, 0], rb.at[j, 0], dev(x_=m4(x + (2 if j >= 2 else s))))
        sb[j, 1] = wgf[j, 1].astype(BF)
        second = remote(sb.at[j, 1], rb.at[j, 1], dev(x_=m4(x - s)))
        xs[j] = [first, second]

    def xs_second(j):
        value = wgf[j, 2]
        if j < 2:
            xs[j][0].wait_recv()
            value = value + rb[j, 0].astype(F32)
        sb[j, 2] = value.astype(BF)
        xs[j].append(remote(sb.at[j, 2], rb.at[j, 2], dev(x_=m4(x + s))))

    def xs_end(j):
        xs[j][1].wait_recv()
        xs[j][2].wait_recv()
        value = wgf[j, 3] + rb[j, 1].astype(F32) + rb[j, 2].astype(F32)
        if j >= 2:
            xs[j][0].wait_recv()
            value = value + rb[j, 0].astype(F32)
        pz[j] = value

    zs = {}

    def z_send(n, j, before, places):
        value = pz[j]
        if before is not None:
            zs[before].wait_recv()
            value = value + rz[before].astype(F32)
        sz[n] = value.astype(BF)
        zs[n] = remote(sz.at[n], rz.at[n], zring(places * s))

    def scores(h):
        st[h] = (mm_nt(k[:, head(h)], q[:, head(h)]) * mst[...]).astype(BF)

    def local_part(h):
        cols = head(h)
        dh = do[:, cols]
        gw = (mm_nt(dh, v[:, cols]) * ms[...]).astype(BF)
        qacc[:, cols] = mm(gw, k[:, cols])
        gt = (mm_nt(v[:, cols], dh) * mst[...]).astype(BF)
        kacc[:, cols] = mm(gt, q[:, cols])
        vacc[:, cols] = mm(st[h], dh)

    forward_g(0)

    wx[0].wait_recv()
    xb = m4(x - s)
    wx.append(remote(wh.at[zl, xb, lo], wh.at[zl, xb, lo], dev(x_=m4(x + s))))
    wz[0].wait_recv()
    zb = m4(zl - s)
    wz.append(remote(wh.at[zb, x, hi], wh.at[zb, x, hi], zring(s)))

    lk.wait()
    lv.wait()
    for h in range(4):
        kt[h] = k[:, head(h)].T
        s_own[0, head(h)] = mm(kt[h], v[:, head(h)])
    kv = scan_start(0)
    lq.wait()
    for h in range(4):
        qt[h] = q[:, head(h)].T

    wx[1].wait_recv()
    wx[2].wait_recv()
    wzz = [remote(wh.at[zl, :, lo], wh.at[zl, :, lo], zring(d * s)) for d in (1, -1)]
    wz[1].wait_recv()
    wz[2].wait_recv()
    wxx = [remote(wh.at[:, x, hi], wh.at[:, x, hi], dev(x_=m4(x + d * s))) for d in (1, -1)]
    ra.wait_recv()
    for g in range(2):
        for t in range(4):
            att[pl.ds(t * 128, 128), pl.ds(g * 512, 512)] = ab[g, :, pl.ds(t * 128, 128)].T
    scan_x(0, kv)

    forward_g(1)
    finish_g(0)
    weight_part(0)
    xs_first(0)
    scores(0)
    scores(1)
    wzz[0].wait_recv()
    wzz.append(remote(wh.at[zb, :, lo], wh.at[zb, :, lo], zring(s)))
    wxx[0].wait_recv()
    wxx.append(remote(wh.at[:, xb, hi], wh.at[:, xb, hi], dev(x_=m4(x + s))))
    scores(2)
    scores(3)
    forward_g(2)
    scan_z(0, kv)
    finish_g(1)
    weight_part(1)
    xs_first(1)
    xs_second(0)
    for cp in wzz[1:] + wxx[1:]:
        cp.wait_recv()
    grads_part(0)
    grads_part(1)
    forward_g(3)
    scan_h(0, kv, False)
    scan_u(0, kv, False)
    xs_end(0)
    z_send(0, 0, None, -1)
    finish_g(2)
    weight_part(2)
    xs_first(2)
    xs_second(2)
    forward_g(4)
    forward_g(5)
    xs_second(1)
    grads_part(2)
    finish_g(3)
    weight_part(3)
    xs_first(3)
    grads_part(3)
    finish_g(4)
    weight_part(4)
    xs_second(3)
    grads_part(4)
    finish_g(5)
    grads_part(5)
    exchange = remote(dacc.at[oc], drecv, sibling)
    weight_part(5)
    exchange.wait_recv()
    do[...] = (dacc[c] + drecv[...]).astype(BF)
    for h in range(4):
        s_own[1, head(h)] = mm(qt[h], do[:, head(h)])
    qg = scan_start(1)
    scan_x(1, qg)
    xs_end(1)
    z_send(1, 1, 0, -1)
    z_send(2, 1, None, 1)
    xs_end(2)
    z_send(3, 2, None, 3)
    z_send(4, 2, None, -1)
    xs_end(3)
    z_send(6, 3, None, 2)
    local_part(0)
    scan_z(1, qg)
    z_send(5, 3, 1, -2)
    local_part(1)
    local_part(2)
    scan_h(1, qg, True)
    scan_u(1, qg, True)
    local_part(3)
    scan_end(0, kv)
    for h in range(4):
        cols = head(h)
        qo[:, cols] = (qacc[:, cols] + mm_nt(do[:, cols], state[0, cols])).astype(BF)
    lo_ = [local(qo, qo_hbm)]
    scan_end(1, qg)
    for h in range(4):
        cols = head(h)
        ko[:, cols] = (kacc[:, cols] + mm_nt(v[:, cols], state[1, cols])).astype(BF)
    lo_.append(local(ko, ko_hbm))
    for h in range(4):
        cols = head(h)
        vo[:, cols] = (vacc[:, cols] + mm(k[:, cols], state[1, cols])).astype(BF)
    lo_.append(local(vo, vo_hbm))
    for n in (2, 3, 4, 5, 6):
        zs[n].wait_recv()
    total = pz[0]
    for n in (2, 3, 4, 5, 6):
        total = total + rz[n].astype(F32)
    wg[...] = total.T
    lo_.append(local(wg, wg_hbm))
    for cp in lo_:
        cp.wait()
    for cp in sent:
        cp.wait_send()


def place(*refs):
    for n in range(4):
        refs[n + 4][...] = refs[n][...]


def shards(queries, keys, values, attn_out, out_grad, out_weight, block_mask):
    group_len, width = queries.shape[1:]
    seq_len = group_len * lax.axis_size("ctx")
    score_scale = 1.0 / math.sqrt(HEAD * seq_len)
    norm_factor = 1.0 / math.sqrt(seq_len * lax.axis_size("dp"))
    tokens, model = out_grad.shape[1:]
    V = pltpu.VMEM
    square = (group_len, width)
    any_spec = pl.BlockSpec(memory_space=pl.ANY)
    body = lambda *refs: kernel(score_scale, norm_factor, *refs)
    results = tuple(
        jax.ShapeDtypeStruct(shape, kind)
        for shape, kind in ((square, BF), (square, BF), (square, BF), (out_weight.shape, F32)))
    out = pl.pallas_call(
        body,
        out_shape=results,
        in_specs=[any_spec] * 6 + [pl.BlockSpec(memory_space=pltpu.SMEM)],
        out_specs=(any_spec,) * 4,
        scratch_shapes=[
            V(square, BF), V(square, BF), V(square, BF),
            V((4, 128, 512), BF), V((4, 128, 512), BF),
            V((4, 2, 4, 128, 512), BF), V((4, 128, 512), BF),
            V((4, 4, 128, 512), BF),
            V((2, 512, 512), BF), V((512, 1024), BF),
            V(square, F32), V(square, F32), V((4, 512, 512), BF),
            V((2, 512, 512), F32), V(square, F32), V(square, BF),
            V((4, 4, 512, 128), F32), V((4, 3, 512, 128), BF), V((4, 3, 512, 128), BF),
            V((4, 512, 128), F32), V((7, 512, 128), BF), V((7, 512, 128), BF),
            V((2, 512, 128), F32), V((2, 256, 128), F32),
            V((2, 256, 128), BF), V((2, 4, 256, 128), BF), V((2, 8, 64, 128), F32),
            V((2, 64, 128), BF), V((2, 4, 64, 128), BF),
            V((2, 64, 128), F32), V((2, 8, 64, 128), F32),
            V((2, 256, 128), F32), V((2, 512, 128), F32), V((2, 512, 128), BF),
            V(square, F32), V(square, F32), V(square, F32),
            V(square, BF), V(square, BF), V(square, BF), V(out_weight.shape, F32),
            pltpu.SemaphoreType.DMA((48,)),
            pltpu.SemaphoreType.DMA((128,)),
            pltpu.SemaphoreType.DMA((128,)),
        ],
        compiler_params=pltpu.CompilerParams(
            collective_id=0, has_side_effects=True, vmem_limit_bytes=58 << 20),
        name="layer_backward",
    )(queries[0], keys[0], values[0], attn_out[0], out_grad[0], out_weight, block_mask[0, 0])
    out = pl.pallas_call(
        place,
        out_shape=results,
        name="place_results",
    )(*out)
    return out[0][None], out[1][None], out[2][None], out[3]


def solution(mesh):
    placed = (
        P("dp", "ctx", "tsp"),
        P("dp", "ctx", "tsp"),
        P("dp", "ctx", "tsp"),
        P("dp", "ctx", "tsp"),
        P("dp", ("ctx", "tsp"), None),
        P("ctx", "tsp"),
        P("dp", "ctx", None, None),
    )
    return jax.shard_map(
        shards,
        mesh=mesh,
        in_specs=placed,
        out_specs=(
            P("dp", "ctx", "tsp"),
            P("dp", "ctx", "tsp"),
            P("dp", "ctx", "tsp"),
            P("ctx", "tsp"),
        ),
        check_vma=False,
    )
```

```python
import math

import jax
import jax.numpy as jnp
from jax import lax
from jax.experimental import pallas as pl
from jax.experimental.pallas import tpu as pltpu
from jax.sharding import PartitionSpec as P

HEAD = 128
BLK = 64
MESH = pl.DeviceIdType.MESH
BF = jnp.bfloat16
F32 = jnp.float32
NT = (((1,), (1,)), ((), ()))
OFFSETS = (0, 3, 1, 2)
SENDS = ((1,), (2,), (3, 4, 5), (), (), ())
PARTS = ((0, 0, 4), (1, 0, 4), (2, 0, 4), (3, 0, 2), (3, 2, 3), (3, 3, 4))


def mm(a, b):
    return jnp.dot(a, b, preferred_element_type=F32)


def mm_nt(a, b):
    return lax.dot_general(a, b, NT, preferred_element_type=F32)


def kernel(score_scale, norm_factor,
           q_hbm, k_hbm, v_hbm, a_hbm, g_hbm, w_hbm, bm_ref,
           qo_hbm, ko_hbm, vo_hbm, wg_hbm,
           q, k, v, qt, kt, og, gp, wh, ab, att, ms, mst, st,
           dacc, drecv, do, wgf, sb, rb, pz, sz, rz,
           s_own, s_sib, s_low, s_x, r_x, r_q, s_z, r_z, s_u, r_u, s_out, near, state,
           qacc, kacc, vacc, qo, ko, vo, wg, lsem, ssem, rsem):
    i = lax.axis_index("ctx")
    y = lax.axis_index("tsp")
    zh = lax.axis_index("dp")
    c = lax.rem(i, 2)
    x = lax.rem(i // 2, 4)
    zl = i // 8
    oc = 1 - c
    s = 1 - 2 * c

    def dev(zl_=None, x_=None, c_=None, y_=None, zh_=None):
        zl_ = zl if zl_ is None else zl_
        x_ = x if x_ is None else x_
        c_ = c if c_ is None else c_
        y_ = y if y_ is None else y_
        zh_ = zh if zh_ is None else zh_
        return ((zl_ * 4 + x_) * 2 + c_, y_, zh_)

    def m4(e):
        return lax.rem(e + 8, 4)

    def zring(d):
        z = lax.rem(zh * 4 + zl + d + 8, 8)
        return dev(zl_=lax.rem(z, 4), zh_=z // 4)

    sibling = dev(c_=oc)
    count = [0]
    sent = []

    def remote(src, dst, device, when=None):
        n = count[0]
        count[0] += 1
        copy = pltpu.make_async_remote_copy(
            src_ref=src, dst_ref=dst, send_sem=ssem.at[n], recv_sem=rsem.at[n],
            device_id=device, device_id_type=MESH)
        if when is None:
            copy.start()
        else:
            pl.when(when)(copy.start)
        sent.append((copy, when))
        return copy

    lcount = [0]

    def local(src, dst):
        n = lcount[0]
        lcount[0] += 1
        copy = pltpu.make_async_copy(src, dst, lsem.at[n])
        copy.start()
        return copy

    def chunk_of(j, core):
        return m4(zl - (1 - 2 * core) * OFFSETS[j])

    def x_of(p, core):
        side = 1 - 2 * core
        return m4(x + (2, -side, side, 0)[p])

    def load_g(n):
        j, p0, p1 = PARTS[n]
        out = []
        for core, dst in ((c, og.at[j, c, y]), (oc, gp.at[j])):
            kk = chunk_of(j, core)
            for p in range(p0, p1):
                col = pl.multiple_of(((kk * 4 + x_of(p, core)) * 2 + core) * 128, 128)
                out.append(local(g_hbm.at[:, pl.ds(col, 128)], dst.at[:, pl.ds(p * 128, 128)]))
        return out

    lw = local(w_hbm, wh.at[zl, x])
    lg = [load_g(n) for n in range(len(PARTS))]
    lk = local(k_hbm, k)
    lv = local(v_hbm, v)
    lq = local(q_hbm, q)
    la = local(a_hbm, ab.at[c])

    up, down = m4(y + 1), m4(y - 1)
    peers = [sibling]
    for yy in (up, down):
        peers += [dev(y_=yy), dev(y_=yy, c_=oc)]
    peers += [dev(x_=m4(x + d), c_=cc) for d in (1, 2, 3) for cc in (c, oc)]
    peers += [zring(d) for d in (1, -1, 2, -2, 3, -3)]
    barrier = pltpu.get_barrier_semaphore()
    for peer in peers:
        pl.semaphore_signal(barrier, inc=1, device_id=peer, device_id_type=MESH)
    pl.semaphore_wait(barrier, len(peers))

    def send_g(n):
        for cp in lg[n]:
            cp.wait()
        j, p0, p1 = PARTS[n]
        cols = pl.ds(p0 * 128, (p1 - p0) * 128)
        own, other = og.at[j, c, y, :, cols], gp.at[j, :, cols]
        return {
            "same+": remote(own, own, dev(y_=up)),
            "cross-": remote(other, own, dev(y_=down, c_=oc)),
            "cross+": remote(other, own, dev(y_=up, c_=oc)),
            "same-": remote(own, own, dev(y_=down)),
            "sib": remote(other, own, sibling),
        }

    yg = []

    def forward_g(n):
        j, p0, p1 = PARTS[n]
        cols = pl.ds(p0 * 128, (p1 - p0) * 128)
        yc = yg[n]
        yc["same+"].wait_recv()
        a = og.at[j, c, down, :, cols]
        yc["fa"] = remote(a, a, dev(y_=up))
        yc["cross-"].wait_recv()
        b = og.at[j, oc, up, :, cols]
        yc["fb"] = remote(b, b, dev(y_=down))
        for later in SENDS[n]:
            yg.append(send_g(later))

    def finish_g(n):
        for name in ("same-", "cross+", "sib", "fa", "fb"):
            yg[n][name].wait_recv()

    yg.append(send_g(0))

    lw.wait()
    wx = [remote(wh.at[zl, x], wh.at[zl, x], dev(x_=m4(x + d * s))) for d in (1, -1)]

    la.wait()
    ra = remote(ab.at[c], ab.at[c], sibling)

    sub = lax.broadcasted_iota(jnp.int32, (BLK, 128), 0)
    lane = lax.broadcasted_iota(jnp.int32, (BLK, 128), 1)
    left = lane < BLK
    within = jnp.where(left, lane, lane - BLK)

    def gate(a, b):
        return jnp.where(bm_ref[a, b] == 1, score_scale, 0.0).astype(F32)

    def piece(entry_a, entry_b):
        return jnp.where(left, entry_a, entry_b)

    zero = jnp.zeros((BLK, 128), F32)
    causal = jnp.where(sub >= within, score_scale, 0.0).astype(F32)
    anti = jnp.where(sub <= within, score_scale, 0.0).astype(F32)

    def entry(i_, j_, diagonal):
        if j_ > i_:
            return zero
        if j_ == i_:
            return diagonal
        return jnp.full((BLK, 128), gate(i_, j_))

    for r in range(8):
        for t in range(4):
            ms[pl.ds(r * BLK, BLK), pl.ds(t * 128, 128)] = piece(
                entry(r, 2 * t, causal), entry(r, 2 * t + 1, causal))
            mst[pl.ds(r * BLK, BLK), pl.ds(t * 128, 128)] = piece(
                entry(2 * t, r, anti), entry(2 * t + 1, r, anti))

    def head(h):
        return pl.ds(h * HEAD, HEAD)

    here = pl.ds(pl.multiple_of(c * 256, 256), 256)
    there = pl.ds(pl.multiple_of(oc * 256, 256), 256)
    me = 2 * x + c
    row = [(x, oc)] + [(m4(x + d), cc) for d in (1, 2, 3) for cc in (c, oc)]

    def eighth(at):
        return pl.ds(pl.multiple_of(at * 64, 64), 64)

    def farther(a, b, after):
        return a > b if after else a < b

    def scan_start(n):
        s_low[n] = s_own[n].astype(BF)
        out = {"row": [
            remote(s_low.at[n, eighth(2 * xo + co)], r_q.at[n, me], dev(x_=xo, c_=co))
            for xo, co in row]}
        out["sib"] = remote(s_own.at[n, there], s_sib.at[n], sibling)
        return out

    def scan_x(n, cps, after):
        cps["sib"].wait_recv()
        s_x[n] = (s_own[n, here] + s_sib[n]).astype(BF)
        cps["x"] = [
            remote(s_x.at[n], r_x.at[n, x], dev(x_=m4(x + d)), farther(x, m4(x + d), after))
            for d in (1, 2, 3)]

    def scan_z(n, cps, after):
        for cp in cps["row"]:
            cp.wait_recv()
        total = s_own[n, eighth(me)]
        for xo, co in row:
            total = total + r_q[n, 2 * xo + co].astype(F32)
        s_z[n] = total.astype(BF)
        cps["z"] = [
            remote(s_z.at[n], r_z.at[n, zl], dev(zl_=m4(zl + d)), farther(zl, m4(zl + d), after))
            for d in (1, 2, 3)]

    def scan_h(n, cps, after):
        for d, cp in zip((1, 2, 3), cps["x"]):
            pl.when(farther(m4(x - d), x, after))(cp.wait_recv)
        part = jnp.zeros((256, 128), F32)
        for d in (1, 2, 3):
            xo = m4(x + d)
            use = farther(xo, x, after)
            part = part + jnp.where(use, r_x[n, xo].astype(F32), 0.0)
        edge = 0 if after else 1
        s_out[n] = part + jnp.where(oc == edge, s_own[n, here], 0.0)
        cps["half"] = remote(s_out.at[n], near.at[n, here], sibling)
        near[n, here] = part + jnp.where(c == edge, s_sib[n], 0.0)

    def scan_u(n, cps, after):
        for d, cp in zip((1, 2, 3), cps["z"]):
            pl.when(farther(m4(zl - d), zl, after))(cp.wait_recv)
        part = jnp.zeros((64, 128), F32)
        for d in (1, 2, 3):
            zo = m4(zl + d)
            use = farther(zo, zl, after)
            part = part + jnp.where(use, r_z[n, zo].astype(F32), 0.0)
        s_u[n] = part.astype(BF)
        cps["u"] = [remote(s_u.at[n], r_u.at[n, me], dev(x_=xo, c_=co)) for xo, co in row]
        r_u[n, me] = part.astype(BF)

    def scan_end(n, cps):
        cps["half"].wait_recv()
        for cp in cps["u"]:
            cp.wait_recv()
        state[n] = ((near[n] + r_u[n].reshape(512, 128).astype(F32)) * score_scale).astype(BF)

    def weight_part(n):
        j, p0, p1 = PARTS[n]
        rhs = og[j, :, :, :, p0 * 128:p1 * 128].reshape(1024, (p1 - p0) * 128)
        full = mm(att[...], rhs) * norm_factor
        for p in range(p0, p1):
            wgf[j, p] = full[:, (p - p0) * 128:(p - p0 + 1) * 128]

    def grads_part(n):
        j, p0, p1 = PARTS[n]
        kk = chunk_of(j, c)
        rhs = jnp.concatenate([wh[kk, x_of(p, c)] for p in range(p0, p1)], axis=0)
        for g in range(2):
            part = mm(og[j, g, :, :, p0 * 128:p1 * 128].reshape(512, (p1 - p0) * 128), rhs)
            if n == 0:
                dacc[g] = part
            else:
                dacc[g] = dacc[g] + part

    xs = {}

    def xs_first(j):
        sb[j, 0] = wgf[j, 0].astype(BF)
        first = remote(sb.at[j, 0], rb.at[j, 0], dev(x_=m4(x + (2 if j >= 2 else s))))
        sb[j, 1] = wgf[j, 1].astype(BF)
        second = remote(sb.at[j, 1], rb.at[j, 1], dev(x_=m4(x - s)))
        xs[j] = [first, second]

    def xs_second(j):
        value = wgf[j, 2]
        if j < 2:
            xs[j][0].wait_recv()
            value = value + rb[j, 0].astype(F32)
        sb[j, 2] = value.astype(BF)
        xs[j].append(remote(sb.at[j, 2], rb.at[j, 2], dev(x_=m4(x + s))))

    def xs_end(j):
        xs[j][1].wait_recv()
        xs[j][2].wait_recv()
        value = wgf[j, 3] + rb[j, 1].astype(F32) + rb[j, 2].astype(F32)
        if j >= 2:
            xs[j][0].wait_recv()
            value = value + rb[j, 0].astype(F32)
        pz[j] = value

    zs = {}

    def z_send(n, j, before, places):
        value = pz[j]
        if before is not None:
            zs[before].wait_recv()
            value = value + rz[before].astype(F32)
        sz[n] = value.astype(BF)
        zs[n] = remote(sz.at[n], rz.at[n], zring(places * s))

    def scores(h):
        st[h] = (mm_nt(k[:, head(h)], q[:, head(h)]) * mst[...]).astype(BF)

    def local_part(h):
        cols = head(h)
        dh = do[:, cols]
        gw = (mm_nt(dh, v[:, cols]) * ms[...]).astype(BF)
        qacc[:, cols] = mm(gw, k[:, cols])
        gt = (mm_nt(v[:, cols], dh) * mst[...]).astype(BF)
        kacc[:, cols] = mm(gt, q[:, cols])
        vacc[:, cols] = mm(st[h], dh)

    forward_g(0)

    wx[0].wait_recv()
    xb = m4(x - s)
    wx.append(remote(wh.at[zl, xb], wh.at[zl, xb], dev(x_=m4(x + s))))
    zb = m4(zl - s)

    lk.wait()
    lv.wait()
    for h in range(4):
        kt[h] = k[:, head(h)].T
        s_own[0, head(h)] = mm(kt[h], v[:, head(h)])
    kv = scan_start(0)
    lq.wait()
    for h in range(4):
        qt[h] = q[:, head(h)].T

    wx[1].wait_recv()
    wx[2].wait_recv()
    wz = [remote(wh.at[zl], wh.at[zl], zring(d * s)) for d in (1, -1)]
    ra.wait_recv()
    for g in range(2):
        for t in range(4):
            att[pl.ds(t * 128, 128), pl.ds(g * 512, 512)] = ab[g, :, pl.ds(t * 128, 128)].T
    scan_x(0, kv, False)

    forward_g(1)
    finish_g(0)
    weight_part(0)
    xs_first(0)
    scores(0)
    scores(1)
    scores(2)
    scores(3)
    forward_g(2)
    wz[0].wait_recv()
    wz.append(remote(wh.at[zb], wh.at[zb], zring(s)))
    scan_z(0, kv, False)
    finish_g(1)
    weight_part(1)
    xs_first(1)
    xs_second(0)
    forward_g(3)
    for cp in wz[1:]:
        cp.wait_recv()
    grads_part(0)
    grads_part(1)
    scan_h(0, kv, False)
    scan_u(0, kv, False)
    xs_end(0)
    z_send(0, 0, None, -1)
    finish_g(2)
    weight_part(2)
    xs_second(1)
    xs_first(2)
    xs_second(2)
    forward_g(4)
    forward_g(5)
    grads_part(2)
    finish_g(3)
    weight_part(3)
    xs_first(3)
    grads_part(3)
    finish_g(4)
    weight_part(4)
    xs_second(3)
    grads_part(4)
    finish_g(5)
    grads_part(5)
    exchange = remote(dacc.at[oc], drecv, sibling)
    weight_part(5)
    xs_end(1)
    z_send(1, 1, 0, -1)
    z_send(2, 1, None, 1)
    xs_end(2)
    z_send(3, 2, None, 3)
    z_send(4, 2, None, -1)
    exchange.wait_recv()
    do[...] = (dacc[c] + drecv[...]).astype(BF)
    for h in range(4):
        s_own[1, head(h)] = mm(qt[h], do[:, head(h)])
    qg = scan_start(1)
    scan_x(1, qg, True)
    local_part(0)
    scan_z(1, qg, True)
    xs_end(3)
    z_send(5, 3, 1, -2)
    z_send(6, 3, None, 2)
    local_part(1)
    local_part(2)
    scan_h(1, qg, True)
    scan_u(1, qg, True)
    local_part(3)
    scan_end(0, kv)
    for h in range(4):
        cols = head(h)
        qo[:, cols] = (qacc[:, cols] + mm_nt(do[:, cols], state[0, cols])).astype(BF)
    lo_ = [local(qo, qo_hbm)]
    scan_end(1, qg)
    for h in range(4):
        cols = head(h)
        ko[:, cols] = (kacc[:, cols] + mm_nt(v[:, cols], state[1, cols])).astype(BF)
    lo_.append(local(ko, ko_hbm))
    for h in range(4):
        cols = head(h)
        vo[:, cols] = (vacc[:, cols] + mm(k[:, cols], state[1, cols])).astype(BF)
    lo_.append(local(vo, vo_hbm))
    for n in (2, 3, 4, 5, 6):
        zs[n].wait_recv()
    total = pz[0]
    for n in (2, 3, 4, 5, 6):
        total = total + rz[n].astype(F32)
    wg[...] = total.T
    lo_.append(local(wg, wg_hbm))
    for cp in lo_:
        cp.wait()
    for cp, when in sent:
        if when is None:
            cp.wait_send()
        else:
            pl.when(when)(cp.wait_send)


def place(*refs):
    for n in range(4):
        refs[n + 4][...] = refs[n][...]


def shards(queries, keys, values, attn_out, out_grad, out_weight, block_mask):
    group_len, width = queries.shape[1:]
    seq_len = group_len * lax.axis_size("ctx")
    score_scale = 1.0 / math.sqrt(HEAD * seq_len)
    norm_factor = 1.0 / math.sqrt(seq_len * lax.axis_size("dp"))
    tokens, model = out_grad.shape[1:]
    V = pltpu.VMEM
    square = (group_len, width)
    any_spec = pl.BlockSpec(memory_space=pl.ANY)
    body = lambda *refs: kernel(score_scale, norm_factor, *refs)
    results = tuple(
        jax.ShapeDtypeStruct(shape, kind)
        for shape, kind in ((square, BF), (square, BF), (square, BF), (out_weight.shape, F32)))
    out = pl.pallas_call(
        body,
        out_shape=results,
        in_specs=[any_spec] * 6 + [pl.BlockSpec(memory_space=pltpu.SMEM)],
        out_specs=(any_spec,) * 4,
        scratch_shapes=[
            V(square, BF), V(square, BF), V(square, BF),
            V((4, 128, 512), BF), V((4, 128, 512), BF),
            V((4, 2, 4, 128, 512), BF), V((4, 128, 512), BF),
            V((4, 4, 128, 512), BF),
            V((2, 512, 512), BF), V((512, 1024), BF),
            V(square, F32), V(square, F32), V((4, 512, 512), BF),
            V((2, 512, 512), F32), V(square, F32), V(square, BF),
            V((4, 4, 512, 128), F32), V((4, 3, 512, 128), BF), V((4, 3, 512, 128), BF),
            V((4, 512, 128), F32), V((7, 512, 128), BF), V((7, 512, 128), BF),
            V((2, 512, 128), F32), V((2, 256, 128), F32), V((2, 512, 128), BF),
            V((2, 256, 128), BF), V((2, 4, 256, 128), BF), V((2, 8, 64, 128), BF),
            V((2, 64, 128), BF), V((2, 4, 64, 128), BF),
            V((2, 64, 128), BF), V((2, 8, 64, 128), BF),
            V((2, 256, 128), F32), V((2, 512, 128), F32), V((2, 512, 128), BF),
            V(square, F32), V(square, F32), V(square, F32),
            V(square, BF), V(square, BF), V(square, BF), V(out_weight.shape, F32),
            pltpu.SemaphoreType.DMA((48,)),
            pltpu.SemaphoreType.DMA((128,)),
            pltpu.SemaphoreType.DMA((128,)),
        ],
        compiler_params=pltpu.CompilerParams(
            collective_id=0, has_side_effects=True, vmem_limit_bytes=58 << 20),
        name="layer_backward",
    )(queries[0], keys[0], values[0], attn_out[0], out_grad[0], out_weight, block_mask[0, 0])
    out = pl.pallas_call(
        place,
        out_shape=results,
        name="place_results",
    )(*out)
    return out[0][None], out[1][None], out[2][None], out[3]


def solution(mesh):
    placed = (
        P("dp", "ctx", "tsp"),
        P("dp", "ctx", "tsp"),
        P("dp", "ctx", "tsp"),
        P("dp", "ctx", "tsp"),
        P("dp", ("ctx", "tsp"), None),
        P("ctx", "tsp"),
        P("dp", "ctx", None, None),
    )
    return jax.shard_map(
        shards,
        mesh=mesh,
        in_specs=placed,
        out_specs=(
            P("dp", "ctx", "tsp"),
            P("dp", "ctx", "tsp"),
            P("dp", "ctx", "tsp"),
            P("ctx", "tsp"),
        ),
        check_vma=False,
    )
```

```python
import math

import jax
import jax.numpy as jnp
from jax import lax
from jax.experimental import pallas as pl
from jax.experimental.pallas import tpu as pltpu
from jax.sharding import PartitionSpec as P

HEAD = 128
BLK = 64
MESH = pl.DeviceIdType.MESH
BF = jnp.bfloat16
F32 = jnp.float32
NT = (((1,), (1,)), ((), ()))
OFFSETS = (0, 3, 1, 2)
SENDS = ((1,), (2,), (3, 4, 5), (), (), ())
PARTS = ((0, 0, 4), (1, 0, 4), (2, 0, 4), (3, 0, 2), (3, 2, 3), (3, 3, 4))


def mm(a, b):
    return jnp.dot(a, b, preferred_element_type=F32)


def mm_nt(a, b):
    return lax.dot_general(a, b, NT, preferred_element_type=F32)


def kernel(score_scale, norm_factor,
           q_hbm, k_hbm, v_hbm, a_hbm, g_hbm, w_hbm, bm_ref,
           qo_hbm, ko_hbm, vo_hbm, wg_hbm,
           q, k, v, qt, kt, og, gp, wh, ab, att, ms, mst, st,
           dacc, drecv, do, wgf, sb, rb, pz, sz, rz,
           s_own, s_sib, s_low, s_x, r_x, r_q, s_z, r_z, s_u, r_u, s_out, near, state,
           qacc, kacc, vacc, qo, ko, vo, wg, lsem, ssem, rsem):
    i = lax.axis_index("ctx")
    y = lax.axis_index("tsp")
    zh = lax.axis_index("dp")
    c = lax.rem(i, 2)
    x = lax.rem(i // 2, 4)
    zl = i // 8
    oc = 1 - c
    s = 1 - 2 * c

    def dev(zl_=None, x_=None, c_=None, y_=None, zh_=None):
        zl_ = zl if zl_ is None else zl_
        x_ = x if x_ is None else x_
        c_ = c if c_ is None else c_
        y_ = y if y_ is None else y_
        zh_ = zh if zh_ is None else zh_
        return ((zl_ * 4 + x_) * 2 + c_, y_, zh_)

    def m4(e):
        return lax.rem(e + 8, 4)

    def zring(d):
        z = lax.rem(zh * 4 + zl + d + 8, 8)
        return dev(zl_=lax.rem(z, 4), zh_=z // 4)

    sibling = dev(c_=oc)
    count = [0]
    sent = []

    def remote(src, dst, device, when=None):
        n = count[0]
        count[0] += 1
        copy = pltpu.make_async_remote_copy(
            src_ref=src, dst_ref=dst, send_sem=ssem.at[n], recv_sem=rsem.at[n],
            device_id=device, device_id_type=MESH)
        if when is None:
            copy.start()
        else:
            pl.when(when)(copy.start)
        sent.append((copy, when))
        return copy

    lcount = [0]

    def local(src, dst):
        n = lcount[0]
        lcount[0] += 1
        copy = pltpu.make_async_copy(src, dst, lsem.at[n])
        copy.start()
        return copy

    def chunk_of(j, core):
        return m4(zl - (1 - 2 * core) * OFFSETS[j])

    def x_of(p, core):
        side = 1 - 2 * core
        return m4(x + (2, -side, side, 0)[p])

    def load_g(n):
        j, p0, p1 = PARTS[n]
        out = []
        for core, dst in ((c, og.at[j, c, y]), (oc, gp.at[j])):
            kk = chunk_of(j, core)
            for p in range(p0, p1):
                col = pl.multiple_of(((kk * 4 + x_of(p, core)) * 2 + core) * 128, 128)
                out.append(local(g_hbm.at[:, pl.ds(col, 128)], dst.at[:, pl.ds(p * 128, 128)]))
        return out

    lw = local(w_hbm, wh.at[zl, x])
    lg = [load_g(n) for n in range(len(PARTS))]
    lk = local(k_hbm, k)
    lv = local(v_hbm, v)
    lq = local(q_hbm, q)
    la = local(a_hbm, ab.at[c])

    up, down = m4(y + 1), m4(y - 1)
    peers = [sibling]
    for yy in (up, down):
        peers += [dev(y_=yy), dev(y_=yy, c_=oc)]
    peers += [dev(x_=m4(x + d), c_=cc) for d in (1, 2, 3) for cc in (c, oc)]
    peers += [zring(d) for d in (1, -1, 2, -2, 3, -3)]
    barrier = pltpu.get_barrier_semaphore()
    for peer in peers:
        pl.semaphore_signal(barrier, inc=1, device_id=peer, device_id_type=MESH)
    pl.semaphore_wait(barrier, len(peers))

    def send_g(n):
        for cp in lg[n]:
            cp.wait()
        j, p0, p1 = PARTS[n]
        cols = pl.ds(p0 * 128, (p1 - p0) * 128)
        own, other = og.at[j, c, y, :, cols], gp.at[j, :, cols]
        return {
            "same+": remote(own, own, dev(y_=up)),
            "cross-": remote(other, own, dev(y_=down, c_=oc)),
            "cross+": remote(other, own, dev(y_=up, c_=oc)),
            "same-": remote(own, own, dev(y_=down)),
            "sib": remote(other, own, sibling),
        }

    yg = []

    def forward_g(n):
        j, p0, p1 = PARTS[n]
        cols = pl.ds(p0 * 128, (p1 - p0) * 128)
        yc = yg[n]
        yc["same+"].wait_recv()
        a = og.at[j, c, down, :, cols]
        yc["fa"] = remote(a, a, dev(y_=up))
        yc["cross-"].wait_recv()
        b = og.at[j, oc, up, :, cols]
        yc["fb"] = remote(b, b, dev(y_=down))
        for later in SENDS[n]:
            yg.append(send_g(later))

    def finish_g(n):
        for name in ("same-", "cross+", "sib", "fa", "fb"):
            yg[n][name].wait_recv()

    yg.append(send_g(0))

    lw.wait()
    wx = [remote(wh.at[zl, x], wh.at[zl, x], dev(x_=m4(x + d * s))) for d in (1, -1)]

    la.wait()
    ra = remote(ab.at[c], ab.at[c], sibling)

    sub = lax.broadcasted_iota(jnp.int32, (BLK, 128), 0)
    lane = lax.broadcasted_iota(jnp.int32, (BLK, 128), 1)
    left = lane < BLK
    within = jnp.where(left, lane, lane - BLK)

    def gate(a, b):
        return jnp.where(bm_ref[a, b] == 1, score_scale, 0.0).astype(F32)

    def piece(entry_a, entry_b):
        return jnp.where(left, entry_a, entry_b)

    zero = jnp.zeros((BLK, 128), F32)
    causal = jnp.where(sub >= within, score_scale, 0.0).astype(F32)
    anti = jnp.where(sub <= within, score_scale, 0.0).astype(F32)

    def entry(i_, j_, diagonal):
        if j_ > i_:
            return zero
        if j_ == i_:
            return diagonal
        return jnp.full((BLK, 128), gate(i_, j_))

    for r in range(8):
        for t in range(4):
            ms[pl.ds(r * BLK, BLK), pl.ds(t * 128, 128)] = piece(
                entry(r, 2 * t, causal), entry(r, 2 * t + 1, causal))
            mst[pl.ds(r * BLK, BLK), pl.ds(t * 128, 128)] = piece(
                entry(2 * t, r, anti), entry(2 * t + 1, r, anti))

    def head(h):
        return pl.ds(h * HEAD, HEAD)

    here = pl.ds(pl.multiple_of(c * 256, 256), 256)
    there = pl.ds(pl.multiple_of(oc * 256, 256), 256)
    me = 2 * x + c
    row = [(x, oc)] + [(m4(x + d), cc) for d in (1, 2, 3) for cc in (c, oc)]

    def eighth(at):
        return pl.ds(pl.multiple_of(at * 64, 64), 64)

    def farther(a, b, after):
        return a > b if after else a < b

    def scan_start(n):
        s_low[n] = s_own[n].astype(BF)
        out = {"row": [
            remote(s_low.at[n, eighth(2 * xo + co)], r_q.at[n, me], dev(x_=xo, c_=co))
            for xo, co in row]}
        out["sib"] = remote(s_own.at[n, there], s_sib.at[n], sibling)
        return out

    def scan_x(n, cps, after):
        cps["sib"].wait_recv()
        s_x[n] = (s_own[n, here] + s_sib[n]).astype(BF)
        cps["x"] = [
            remote(s_x.at[n], r_x.at[n, x], dev(x_=m4(x + d)), farther(x, m4(x + d), after))
            for d in (1, 2, 3)]

    def scan_z(n, cps, after):
        for cp in cps["row"]:
            cp.wait_recv()
        total = s_own[n, eighth(me)]
        for xo, co in row:
            total = total + r_q[n, 2 * xo + co].astype(F32)
        s_z[n] = total.astype(BF)
        cps["z"] = [
            remote(s_z.at[n], r_z.at[n, zl], dev(zl_=m4(zl + d)), farther(zl, m4(zl + d), after))
            for d in (1, 2, 3)]

    def scan_h(n, cps, after):
        for d, cp in zip((1, 2, 3), cps["x"]):
            pl.when(farther(m4(x - d), x, after))(cp.wait_recv)
        part = jnp.zeros((256, 128), F32)
        for d in (1, 2, 3):
            xo = m4(x + d)
            use = farther(xo, x, after)
            part = part + jnp.where(use, r_x[n, xo].astype(F32), 0.0)
        edge = 0 if after else 1
        s_out[n] = part + jnp.where(oc == edge, s_own[n, here], 0.0)
        cps["half"] = remote(s_out.at[n], near.at[n, here], sibling)
        near[n, here] = part + jnp.where(c == edge, s_sib[n], 0.0)

    def scan_u(n, cps, after):
        for d, cp in zip((1, 2, 3), cps["z"]):
            pl.when(farther(m4(zl - d), zl, after))(cp.wait_recv)
        part = jnp.zeros((64, 128), F32)
        for d in (1, 2, 3):
            zo = m4(zl + d)
            use = farther(zo, zl, after)
            part = part + jnp.where(use, r_z[n, zo].astype(F32), 0.0)
        s_u[n] = part.astype(BF)
        cps["u"] = [remote(s_u.at[n], r_u.at[n, me], dev(x_=xo, c_=co)) for xo, co in row]
        r_u[n, me] = part.astype(BF)

    def scan_end(n, cps):
        cps["half"].wait_recv()
        for cp in cps["u"]:
            cp.wait_recv()
        state[n] = ((near[n] + r_u[n].reshape(512, 128).astype(F32)) * score_scale).astype(BF)

    def weight_part(n):
        j, p0, p1 = PARTS[n]
        rhs = og[j, :, :, :, p0 * 128:p1 * 128].reshape(1024, (p1 - p0) * 128)
        full = mm(att[...], rhs) * norm_factor
        for p in range(p0, p1):
            wgf[j, p] = full[:, (p - p0) * 128:(p - p0 + 1) * 128]

    def grads_part(n):
        j, p0, p1 = PARTS[n]
        kk = chunk_of(j, c)
        rhs = jnp.concatenate([wh[kk, x_of(p, c)] for p in range(p0, p1)], axis=0)
        for g in range(2):
            part = mm(og[j, g, :, :, p0 * 128:p1 * 128].reshape(512, (p1 - p0) * 128), rhs)
            if n == 0:
                dacc[g] = part
            else:
                dacc[g] = dacc[g] + part

    xs = {}

    def xs_first(j):
        sb[j, 0] = wgf[j, 0].astype(BF)
        first = remote(sb.at[j, 0], rb.at[j, 0], dev(x_=m4(x + (2 if j >= 2 else s))))
        sb[j, 1] = wgf[j, 1].astype(BF)
        second = remote(sb.at[j, 1], rb.at[j, 1], dev(x_=m4(x - s)))
        xs[j] = [first, second]

    def xs_second(j):
        value = wgf[j, 2]
        if j < 2:
            xs[j][0].wait_recv()
            value = value + rb[j, 0].astype(F32)
        sb[j, 2] = value.astype(BF)
        xs[j].append(remote(sb.at[j, 2], rb.at[j, 2], dev(x_=m4(x + s))))

    def xs_end(j):
        xs[j][1].wait_recv()
        xs[j][2].wait_recv()
        value = wgf[j, 3] + rb[j, 1].astype(F32) + rb[j, 2].astype(F32)
        if j >= 2:
            xs[j][0].wait_recv()
            value = value + rb[j, 0].astype(F32)
        pz[j] = value

    zs = {}

    def z_send(n, j, before, places):
        value = pz[j]
        if before is not None:
            zs[before].wait_recv()
            value = value + rz[before].astype(F32)
        sz[n] = value.astype(BF)
        zs[n] = remote(sz.at[n], rz.at[n], zring(places * s))

    def scores(h):
        st[h] = (mm_nt(k[:, head(h)], q[:, head(h)]) * mst[...]).astype(BF)

    def local_part(h):
        cols = head(h)
        dh = do[:, cols]
        gw = (mm_nt(dh, v[:, cols]) * ms[...]).astype(BF)
        qacc[:, cols] = mm(gw, k[:, cols])
        gt = (mm_nt(v[:, cols], dh) * mst[...]).astype(BF)
        kacc[:, cols] = mm(gt, q[:, cols])
        vacc[:, cols] = mm(st[h], dh)

    forward_g(0)

    wx[0].wait_recv()
    xb = m4(x - s)
    wx.append(remote(wh.at[zl, xb], wh.at[zl, xb], dev(x_=m4(x + s))))
    zb = m4(zl - s)

    lk.wait()
    lv.wait()
    for h in range(4):
        kt[h] = k[:, head(h)].T
        s_own[0, head(h)] = mm(kt[h], v[:, head(h)])
    kv = scan_start(0)
    lq.wait()
    for h in range(4):
        qt[h] = q[:, head(h)].T

    wx[1].wait_recv()
    wx[2].wait_recv()
    wz = [remote(wh.at[zl], wh.at[zl], zring(d * s)) for d in (1, -1)]
    ra.wait_recv()
    for g in range(2):
        for t in range(4):
            att[pl.ds(t * 128, 128), pl.ds(g * 512, 512)] = ab[g, :, pl.ds(t * 128, 128)].T
    scan_x(0, kv, False)

    forward_g(1)
    finish_g(0)
    weight_part(0)
    xs_first(0)
    scores(0)
    scores(1)
    scores(2)
    scores(3)
    forward_g(2)
    wz[0].wait_recv()
    wz.append(remote(wh.at[zb], wh.at[zb], zring(s)))
    scan_z(0, kv, False)
    finish_g(1)
    weight_part(1)
    xs_first(1)
    xs_second(0)
    forward_g(3)
    for cp in wz[1:]:
        cp.wait_recv()
    grads_part(0)
    grads_part(1)
    scan_h(0, kv, False)
    scan_u(0, kv, False)
    xs_end(0)
    z_send(0, 0, None, -1)
    finish_g(2)
    weight_part(2)
    xs_second(1)
    xs_first(2)
    xs_second(2)
    forward_g(4)
    forward_g(5)
    grads_part(2)
    finish_g(3)
    weight_part(3)
    xs_first(3)
    grads_part(3)
    finish_g(4)
    weight_part(4)
    xs_second(3)
    grads_part(4)
    finish_g(5)
    grads_part(5)
    exchange = remote(dacc.at[oc], drecv, sibling)
    weight_part(5)
    xs_end(1)
    z_send(1, 1, 0, -1)
    z_send(2, 1, None, 1)
    xs_end(2)
    z_send(3, 2, None, 3)
    z_send(4, 2, None, -1)
    exchange.wait_recv()
    do[...] = (dacc[c] + drecv[...]).astype(BF)
    for h in range(4):
        s_own[1, head(h)] = mm(qt[h], do[:, head(h)])
    qg = scan_start(1)
    scan_x(1, qg, True)
    local_part(0)
    scan_z(1, qg, True)
    xs_end(3)
    z_send(5, 3, 1, -2)
    z_send(6, 3, None, 2)
    local_part(1)
    scan_h(1, qg, True)
    scan_u(1, qg, True)
    local_part(2)
    local_part(3)
    scan_end(0, kv)
    for h in range(4):
        cols = head(h)
        qo[:, cols] = (qacc[:, cols] + mm_nt(do[:, cols], state[0, cols])).astype(BF)
    lo_ = [local(qo, qo_hbm)]
    scan_end(1, qg)
    for h in range(4):
        cols = head(h)
        ko[:, cols] = (kacc[:, cols] + mm_nt(v[:, cols], state[1, cols])).astype(BF)
    lo_.append(local(ko, ko_hbm))
    for h in range(4):
        cols = head(h)
        vo[:, cols] = (vacc[:, cols] + mm(k[:, cols], state[1, cols])).astype(BF)
    lo_.append(local(vo, vo_hbm))
    for n in (2, 3, 4, 5, 6):
        zs[n].wait_recv()
    total = pz[0]
    for n in (2, 3, 4, 5, 6):
        total = total + rz[n].astype(F32)
    wg[...] = total.T
    lo_.append(local(wg, wg_hbm))
    for cp in lo_:
        cp.wait()
    for cp, when in sent:
        if when is None:
            cp.wait_send()
        else:
            pl.when(when)(cp.wait_send)


def place(*refs):
    source, target, held, first, second = refs[:4], refs[4:8], refs[8:12], refs[12], refs[13]
    arriving = [pltpu.make_async_copy(source[n], held[n], first.at[n]) for n in range(4)]
    leaving = [pltpu.make_async_copy(held[n], target[n], second.at[n]) for n in range(4)]
    for cp in arriving:
        cp.start()
    for n in range(4):
        arriving[n].wait()
        leaving[n].start()
    for cp in leaving:
        cp.wait()


def shards(queries, keys, values, attn_out, out_grad, out_weight, block_mask):
    group_len, width = queries.shape[1:]
    seq_len = group_len * lax.axis_size("ctx")
    score_scale = 1.0 / math.sqrt(HEAD * seq_len)
    norm_factor = 1.0 / math.sqrt(seq_len * lax.axis_size("dp"))
    tokens, model = out_grad.shape[1:]
    V = pltpu.VMEM
    square = (group_len, width)
    any_spec = pl.BlockSpec(memory_space=pl.ANY)
    body = lambda *refs: kernel(score_scale, norm_factor, *refs)
    results = tuple(
        jax.ShapeDtypeStruct(shape, kind)
        for shape, kind in ((square, BF), (square, BF), (square, BF), (out_weight.shape, F32)))
    out = pl.pallas_call(
        body,
        out_shape=results,
        in_specs=[any_spec] * 6 + [pl.BlockSpec(memory_space=pltpu.SMEM)],
        out_specs=(any_spec,) * 4,
        scratch_shapes=[
            V(square, BF), V(square, BF), V(square, BF),
            V((4, 128, 512), BF), V((4, 128, 512), BF),
            V((4, 2, 4, 128, 512), BF), V((4, 128, 512), BF),
            V((4, 4, 128, 512), BF),
            V((2, 512, 512), BF), V((512, 1024), BF),
            V(square, F32), V(square, F32), V((4, 512, 512), BF),
            V((2, 512, 512), F32), V(square, F32), V(square, BF),
            V((4, 4, 512, 128), F32), V((4, 3, 512, 128), BF), V((4, 3, 512, 128), BF),
            V((4, 512, 128), F32), V((7, 512, 128), BF), V((7, 512, 128), BF),
            V((2, 512, 128), F32), V((2, 256, 128), F32), V((2, 512, 128), BF),
            V((2, 256, 128), BF), V((2, 4, 256, 128), BF), V((2, 8, 64, 128), BF),
            V((2, 64, 128), BF), V((2, 4, 64, 128), BF),
            V((2, 64, 128), BF), V((2, 8, 64, 128), BF),
            V((2, 256, 128), F32), V((2, 512, 128), F32), V((2, 512, 128), BF),
            V(square, F32), V(square, F32), V(square, F32),
            V(square, BF), V(square, BF), V(square, BF), V(out_weight.shape, F32),
            pltpu.SemaphoreType.DMA((48,)),
            pltpu.SemaphoreType.DMA((128,)),
            pltpu.SemaphoreType.DMA((128,)),
        ],
        compiler_params=pltpu.CompilerParams(
            collective_id=0, has_side_effects=True, vmem_limit_bytes=58 << 20),
        name="layer_backward",
    )(queries[0], keys[0], values[0], attn_out[0], out_grad[0], out_weight, block_mask[0, 0])
    out = pl.pallas_call(
        place,
        out_shape=results,
        in_specs=[any_spec] * 4,
        out_specs=(any_spec,) * 4,
        scratch_shapes=[
            V(square, BF), V(square, BF), V(square, BF), V(out_weight.shape, F32),
            pltpu.SemaphoreType.DMA((4,)), pltpu.SemaphoreType.DMA((4,)),
        ],
        name="place_results",
    )(*out)
    return out[0][None], out[1][None], out[2][None], out[3]


def solution(mesh):
    placed = (
        P("dp", "ctx", "tsp"),
        P("dp", "ctx", "tsp"),
        P("dp", "ctx", "tsp"),
        P("dp", "ctx", "tsp"),
        P("dp", ("ctx", "tsp"), None),
        P("ctx", "tsp"),
        P("dp", "ctx", None, None),
    )
    return jax.shard_map(
        shards,
        mesh=mesh,
        in_specs=placed,
        out_specs=(
            P("dp", "ctx", "tsp"),
            P("dp", "ctx", "tsp"),
            P("dp", "ctx", "tsp"),
            P("ctx", "tsp"),
        ),
        check_vma=False,
    )
```
